32 devices in a mesh: dp: 4 (over y, x), seq: 4 (over z), heads: 2 (over core).
Axes of the slice: x: 2, y: 2, z: 4, core: 2. Of those that a mesh axis runs over, the one named last changes fastest.
Arguments:
- hidden_in: bfloat16 [16, 1024, 768], P('dp', 'seq'), may hold values from -6 to 6
- out_grad: bfloat16 [16, 1024, 768], P('dp', 'seq'), may hold values from -6 to 6
- doc_starts: int32 [16, 1024], P('dp', 'seq'), may hold values from 0 to 1, as said below
- norm_gain: bfloat16 [768], P(('dp', 'seq', 'heads')), may hold values from 0.5 to 1.5
- w_z: bfloat16 [768, 1536], P(('dp', 'seq'), 'heads'), may hold values from -0.21875 to 0.21875
- w_x: bfloat16 [768, 1536], P(('dp', 'seq'), 'heads'), may hold values from -0.21875 to 0.21875
- w_bc: bfloat16 [768, 256], P(('dp', 'seq', 'heads')), may hold values from -0.21875 to 0.21875
- w_dt: bfloat16 [768, 24], P(('dp', 'seq'), 'heads'), may hold values from -0.21875 to 0.21875
- conv_x: bfloat16 [4, 24, 64], P(None, 'heads', ('dp', 'seq')), may hold values from -3 to 3
- conv_bias_x: bfloat16 [24, 64], P('heads', ('dp', 'seq')), may hold values from -0.5 to 0.5
- conv_bc: bfloat16 [4, 256], P(None, ('dp', 'seq', 'heads')), may hold values from -3 to 3
- conv_bias_bc: bfloat16 [256], P(('dp', 'seq', 'heads')), may hold values from -0.5 to 0.5
- dt_bias: float32 [24], P('heads'), may hold values from -6.5 to -3.5
- a_log: float32 [24], P('heads'), may hold values from -4.5 to 2
- d_skip: float32 [24], P('heads'), may hold values from 0.5 to 2
- gated_gain: bfloat16 [24, 64], P('heads', ('dp', 'seq')), may hold values from 0.5 to 1.5
- w_out: bfloat16 [1536, 768], P('heads', ('dp', 'seq')), may hold values from -0.15625 to 0.15625
Outputs:
- block_out: bfloat16 [16, 1024, 768], P('dp', 'seq', 'heads')
- input_grad: float32 [16, 1024, 768], P('dp', 'seq', 'heads')
- grad_norm_gain: float32 [768], P(('dp', 'seq', 'heads'))
- grad_w_z: float32 [768, 1536], P(('dp', 'seq'), 'heads')
- grad_w_x: float32 [768, 1536], P(('dp', 'seq'), 'heads')
- grad_w_bc: float32 [768, 256], P(('dp', 'seq', 'heads'))
- grad_w_dt: float32 [768, 24], P(('dp', 'seq'), 'heads')
- grad_conv_x: float32 [4, 24, 64], P(None, 'heads', ('dp', 'seq'))
- grad_conv_bias_x: float32 [24, 64], P('heads', ('dp', 'seq'))
- grad_conv_bc: float32 [4, 256], P(None, ('dp', 'seq', 'heads'))
- grad_conv_bias_bc: float32 [256], P(('dp', 'seq', 'heads'))
- grad_dt_bias: float32 [24], P('heads')
- grad_a_log: float32 [24], P('heads')
- grad_d_skip: float32 [24], P('heads')
- grad_gated_gain: float32 [24, 64], P('heads', ('dp', 'seq'))
- grad_w_out: float32 [1536, 768], P('heads', ('dp', 'seq'))
The draws below stay inside these ranges and needn't reach their ends.
Inputs may be any that keep to these rules, and one draw needn't show every extreme that they name: `doc_starts`: every sequence has a 1 at position 0.
All inputs are finite; a program needn't handle non-finite values.
Results may differ from the reference program's by a relative error of at most 0.034.
Values may be sent and summed in bfloat16 or wider, within the bound.
No kernel may reach another device: no remote copies, remote signals or barrier semaphores. Data moves between devices by JAX's collectives and lax.ppermute only.
A program may use at most 192 MiB of HBM per device.

```python
import jax
import jax.numpy as jnp
from jax import lax

D = 768
H = 24
P_SIZE = 64
N = 128
K = 4
E = 1536
POS_DEV = 256
DOC_MIN = 200
DOC_MAX = 2000
SEQS = 16
L = 1024
N_HEADS = 2


def draw_doc_starts(key, part):
    most_docs = L // DOC_MIN + 2
    sizes_drawn = jax.random.randint(key, (SEQS, most_docs), DOC_MIN, DOC_MAX + 1, dtype=jnp.int32)
    doc_ends = jnp.cumsum(sizes_drawn, axis=1).astype(jnp.int32)
    begins = jnp.concatenate([jnp.zeros((SEQS, 1), jnp.int32), doc_ends[:, :-1]], axis=1)
    begins = jnp.minimum(begins, L)
    row_index = jnp.broadcast_to(jnp.arange(SEQS, dtype=jnp.int32)[:, None], begins.shape)
    start_flags = jnp.zeros((SEQS, L + 1), jnp.int32).at[row_index, begins].set(1)
    return start_flags[:, :L]


def draw_a_log(key, part):
    values = jax.random.uniform(key, (H,), jnp.float32, -3.0, 2.0)
    return values


def shard_levels(key, extent, split, low, high):
    gain, own = 1.0, jax.random.fold_in(key, 6)
    for position, shards_of in split:
        heights = jnp.exp(jax.random.uniform(jax.random.fold_in(own, position), (shards_of,), jnp.float32, low / len(split), high / len(split)))
        gain = gain * jnp.repeat(heights, extent[position] // shards_of).reshape([-1 if axis == position else 1 for axis in range(len(extent))])
    return gain


def scatter_about(stream_key, shape, scale, bound, pieces=(), kind=jnp.bfloat16):
    level = shard_levels(stream_key, shape, pieces, -0.22, 0.18) if pieces else 1.0
    values = jax.random.normal(stream_key, shape, jnp.float32) * scale * level
    return jnp.minimum(jnp.maximum(values, -bound), bound).astype(kind)


def setup_inputs(seed: int = 0) -> dict:
    splits = jax.random.split(jax.random.key(seed), 18)
    return {
        "hidden_in": scatter_about(splits[0], (SEQS, L, D), 1.0, 6.0, ((0, 4), (1, 4))),
        "out_grad": scatter_about(splits[1], (SEQS, L, D), 1.0, 6.0, ((0, 4), (1, 4))),
        "doc_starts": draw_doc_starts(jax.random.fold_in(splits[17], 71), 0),
        "norm_gain": jnp.clip(1.0 + 0.1 * jax.random.normal(splits[3], (D,), jnp.float32), 0.5, 1.5).astype(jnp.bfloat16),
        "w_z": scatter_about(splits[4], (D, E), D ** -0.5, 0.21875, ((0, 16), (1, 2))),
        "w_x": scatter_about(splits[5], (D, E), D ** -0.5, 0.21875, ((0, 16), (1, 2))),
        "w_bc": scatter_about(splits[6], (D, 2 * N), D ** -0.5, 0.21875, ((0, 32),)),
        "w_dt": scatter_about(splits[7], (D, H), D ** -0.5, 0.21875, ((0, 16), (1, 2))),
        "conv_x": scatter_about(splits[8], (K, H, P_SIZE), K ** -0.5, 3.0, ((1, 2), (2, 16))),
        "conv_bias_x": jnp.clip(jax.random.uniform(splits[9], (H, P_SIZE), jnp.float32, -0.5, 0.5) * shard_levels(splits[9], (H, P_SIZE), ((0, 2), (1, 16)), -0.4, 0.0), -0.5, 0.5).astype(jnp.bfloat16),
        "conv_bc": scatter_about(splits[10], (K, 2 * N), K ** -0.5, 3.0, ((1, 32),)),
        "conv_bias_bc": jnp.clip(jax.random.uniform(splits[11], (2 * N,), jnp.float32, -0.5, 0.5) * shard_levels(splits[11], (2 * N,), ((0, 32),), -0.4, 0.0), -0.5, 0.5).astype(jnp.bfloat16),
        "dt_bias": jnp.clip(-6.5 + 3.0 * jax.random.uniform(splits[12], (H,), jnp.float32) ** shard_levels(splits[12], (H,), ((0, 2),), -0.2, 0.2), -6.5, -3.5),
        "a_log": draw_a_log(jax.random.fold_in(splits[17], 71), 0),
        "d_skip": jnp.clip(0.5 + 1.5 * jax.random.uniform(splits[14], (H,), jnp.float32) ** shard_levels(splits[14], (H,), ((0, 2),), -0.2, 0.2), 0.5, 2.0),
        "gated_gain": jnp.clip(1.0 + 0.1 * jax.random.normal(splits[15], (H, P_SIZE), jnp.float32), 0.5, 1.5).astype(jnp.bfloat16),
        "w_out": scatter_about(splits[16], (E, D), E ** -0.5, 0.15625, ((0, 2), (1, 16))),
    }


epsilon = 1e-05

def contract(pattern, left_op, right_op):
    return jnp.einsum(pattern, left_op.astype(jnp.float32), right_op.astype(jnp.float32), precision=lax.Precision.HIGHEST)

def exact_sum(pattern, left_op, right_op):
    return jnp.einsum(pattern, left_op, right_op, precision=lax.Precision.HIGHEST)

def silu_slope(values, sigmoid_v):
    return sigmoid_v * (1.0 + values * (1.0 - sigmoid_v))

def causal_conv(padded, doc_pad, doc_index, weights, offsets):
    tap_count = weights.shape[0]
    length = doc_index.shape[1]
    result = jnp.zeros((padded.shape[0], length, padded.shape[2]), jnp.float32) + offsets
    for tap_index in range(tap_count):
        source = padded[:, tap_index:tap_index + length].astype(jnp.float32)
        linked = (doc_pad[:, tap_index:tap_index + length] == doc_index).astype(jnp.float32)[..., None]
        result = result + weights[tap_index] * source * linked
    return result

def conv_backward(padded, doc_pad, doc_index, weights, upstream):
    tap_count = weights.shape[0]
    length = doc_index.shape[1]
    back_grad = jnp.zeros(padded.shape, jnp.float32)
    tap_grads = []
    for tap_index in range(tap_count):
        source = padded[:, tap_index:tap_index + length].astype(jnp.float32)
        linked = (doc_pad[:, tap_index:tap_index + length] == doc_index).astype(jnp.float32)[..., None]
        masked = upstream * linked
        tap_grads.append(lax.optimization_barrier(jnp.sum(masked * source, axis=(0, 1))))
        back_grad = back_grad + jnp.pad(weights[tap_index] * masked, ((0, 0), (tap_index, tap_count - 1 - tap_index), (0, 0)))
    return (back_grad, jnp.stack(tap_grads), lax.optimization_barrier(jnp.sum(upstream, axis=(0, 1))))

def small_tables(log_decay, doc_index):
    cumulative = jnp.cumsum(log_decay, axis=1)
    fresh_mask = (doc_index == 0).astype(jnp.float32)
    entry_decay = jnp.exp(cumulative) * fresh_mask[..., None]
    carry_decay = jnp.exp(cumulative[:, -1]) * fresh_mask[:, -1:]
    return (entry_decay, carry_decay)

def block_tables(log_decay, doc_index):
    entry_decay, carry_decay = small_tables(log_decay, doc_index)
    cumulative = jnp.cumsum(log_decay, axis=1)
    length = doc_index.shape[1]
    rows_iota = lax.broadcasted_iota(jnp.int32, (length, length), 0)
    cols_iota = lax.broadcasted_iota(jnp.int32, (length, length), 1)
    linked = ((rows_iota >= cols_iota)[None] & (doc_index[:, :, None] == doc_index[:, None, :]))[:, None]
    cumul_heads = jnp.transpose(cumulative, (0, 2, 1))
    spread = cumul_heads[:, :, :, None] - cumul_heads[:, :, None, :]
    decays = jnp.where(linked, jnp.exp(jnp.where(linked, spread, 0.0)), 0.0)
    closing = (doc_index == doc_index[:, -1:]).astype(jnp.float32)
    tail_decay = jnp.exp(cumulative[:, -1:, :] - cumulative) * closing[..., None]
    return (decays, tail_decay, entry_decay, carry_decay)

def ssd_forward(ssd_input, b_state, c_state, step_size, log_decay, doc_index):
    decays, tail_decay, entry_decay, carry_decay = block_tables(log_decay, doc_index)
    inner_prod = contract('ctn,csn->cts', c_state, b_state)
    step_heads = jnp.transpose(step_size, (0, 2, 1))
    scores = (inner_prod[:, None] * decays * step_heads[:, :, None, :]).astype(jnp.bfloat16)
    local_out = contract('chts,cshp->cthp', scores, ssd_input)
    weighted = (b_state.astype(jnp.float32)[:, :, None, :] * (tail_decay * step_size)[..., None]).astype(jnp.bfloat16)
    state_local = contract('cshp,cshn->chpn', ssd_input, weighted)
    return (local_out, state_local)

def state_entry_grad(grad_bf, c_state, entry_decay):
    entry_c = (entry_decay[..., None] * c_state.astype(jnp.float32)[:, :, None, :]).astype(jnp.bfloat16)
    return contract('cthp,cthn->chpn', grad_bf, entry_c)

def ssd_backward(ssd_input, b_state, c_state, step_size, log_decay, doc_index, grad_bf, state_bf, state_in, grad_out_state):
    decays, tail_decay, entry_decay, carry_decay = block_tables(log_decay, doc_index)
    inner_prod = contract('ctn,csn->cts', c_state, b_state)
    step_heads = jnp.transpose(step_size, (0, 2, 1))
    scores = (inner_prod[:, None] * decays * step_heads[:, :, None, :]).astype(jnp.bfloat16)
    weighted = (b_state.astype(jnp.float32)[:, :, None, :] * (tail_decay * step_size)[..., None]).astype(jnp.bfloat16)
    inter_grad = contract('cthp,chpn->cthn', grad_bf, state_bf)
    grad_cstate = exact_sum('cth,cthn->ctn', entry_decay, inter_grad)
    grad_cumul = exact_sum('ctn,cthn->cth', c_state.astype(jnp.float32), inter_grad) * entry_decay
    score_grad = contract('cthp,cshp->chts', grad_bf, ssd_input)
    grad_input = contract('chts,cthp->cshp', scores, grad_bf)
    masked_grad = score_grad * decays
    inner_grad = exact_sum('chts,chs->cts', masked_grad, step_heads).astype(jnp.bfloat16)
    grad_cstate = grad_cstate + contract('cts,csn->ctn', inner_grad, b_state)
    grad_bstate = contract('cts,ctn->csn', inner_grad, c_state)
    step_part = masked_grad * inner_prod[:, None]
    grad_step = jnp.transpose(lax.optimization_barrier(jnp.sum(step_part, axis=2)), (0, 2, 1))
    cumul_part = step_part * step_heads[:, :, None, :]
    grad_cumul = grad_cumul + jnp.transpose(lax.optimization_barrier(jnp.sum(cumul_part, axis=3)) - lax.optimization_barrier(jnp.sum(cumul_part, axis=2)), (0, 2, 1))
    state_grad_bf = grad_out_state.astype(jnp.bfloat16)
    grad_input = grad_input + contract('cshn,chpn->cshp', weighted, state_grad_bf)
    weight_grad = contract('cshp,chpn->cshn', ssd_input, state_grad_bf)
    state_dot = exact_sum('cshn,csn->csh', weight_grad, b_state.astype(jnp.float32))
    grad_bstate = grad_bstate + exact_sum('cshn,csh->csn', weight_grad, tail_decay * step_size)
    grad_step = grad_step + state_dot * tail_decay
    spent_grad = state_dot * tail_decay * step_size
    end_grad = lax.optimization_barrier(jnp.sum(spent_grad, axis=1)) + carry_decay * exact_sum('chpn,chpn->ch', grad_out_state, state_in)
    grad_cumul = grad_cumul - spent_grad
    grad_cumul = grad_cumul.at[:, -1].add(end_grad)
    grad_log = jnp.flip(jnp.cumsum(jnp.flip(grad_cumul, 1), 1), 1)
    return (grad_input, grad_bstate, grad_cstate, grad_step, grad_log)

def forward_chain(carry_decay, state_local):

    def advance(state_now, members):
        decay_now, local_now = members
        return (decay_now[:, None, None] * state_now + local_now, state_now)
    return lax.scan(advance, jnp.zeros(state_local.shape[1:], jnp.float32), (carry_decay, state_local))[1]

def backward_chain(carry_decay, grad_local):

    def retreat(state_now, members):
        decay_now, local_now = members
        return (local_now + decay_now[:, None, None] * state_now, state_now)
    return lax.scan(retreat, jnp.zeros(grad_local.shape[1:], jnp.float32), (carry_decay, grad_local), reverse=True)[1]

def reference(hidden_in, out_grad, doc_starts, norm_gain, w_z, w_x, w_bc, w_dt, conv_x, conv_bias_x, conv_bc, conv_bias_bc, dt_bias, a_log, d_skip, gated_gain, w_out):
    groups = N_HEADS
    group_heads = H // groups
    group_width = group_heads * P_SIZE
    inner_width = H * P_SIZE
    blocks = L // POS_DEV
    conv_weight = jnp.concatenate([conv_x.reshape(K, inner_width), conv_bc], axis=1).astype(jnp.float32)
    conv_offset = jnp.concatenate([conv_bias_x.reshape(inner_width), conv_bias_bc]).astype(jnp.float32)
    gain_in = norm_gain.astype(jnp.float32)
    gain_gate = gated_gain.reshape(inner_width).astype(jnp.float32)
    decay_rates = jnp.exp(a_log)

    def per_sequence(totals, members):
        hidden, cotangent, starts = members
        hidden_float = hidden.astype(jnp.float32)
        inverse_rms = lax.rsqrt(lax.optimization_barrier(jnp.mean(hidden_float * hidden_float, axis=-1, keepdims=True)) + epsilon)
        normed = (hidden_float * inverse_rms * gain_in).astype(jnp.bfloat16)
        gate_proj = jnp.dot(normed, w_z, preferred_element_type=jnp.float32).astype(jnp.bfloat16)
        input_proj = jnp.dot(normed, w_x, preferred_element_type=jnp.float32).astype(jnp.bfloat16)
        state_proj = jnp.dot(normed, w_bc, preferred_element_type=jnp.float32).astype(jnp.bfloat16)
        step_raw = jnp.dot(normed, w_dt, preferred_element_type=jnp.float32).astype(jnp.bfloat16)
        pre_conv = jnp.concatenate([input_proj, state_proj], axis=1)
        doc_full = jnp.cumsum(starts).astype(jnp.int32)[None]
        doc_pad = jnp.concatenate([jnp.full((1, K - 1), -1, jnp.int32), doc_full], axis=1)
        padded = jnp.concatenate([jnp.zeros((K - 1, pre_conv.shape[1]), jnp.bfloat16), pre_conv], axis=0)[None]
        conv_out = causal_conv(padded, doc_pad, doc_full, conv_weight, conv_offset)[0]
        conv_sigm = jax.nn.sigmoid(conv_out)
        activated = conv_out * conv_sigm
        ssd_input = activated[:, :inner_width].astype(jnp.bfloat16).reshape(blocks, POS_DEV, H, P_SIZE)
        b_state = activated[:, inner_width:inner_width + N].astype(jnp.bfloat16).reshape(blocks, POS_DEV, N)
        c_state = activated[:, inner_width + N:].astype(jnp.bfloat16).reshape(blocks, POS_DEV, N)
        raw_float = (step_raw.astype(jnp.float32) + dt_bias).reshape(blocks, POS_DEV, H)
        step_size = jax.nn.softplus(raw_float)
        log_decay = -step_size * decay_rates
        doc_block = jnp.cumsum(starts.reshape(blocks, POS_DEV), axis=1).astype(jnp.int32)
        kept_state = []
        outputs = []
        for group_index in range(groups):
            head_low = group_index * group_heads
            head_high = head_low + group_heads
            group_input = ssd_input[:, :, head_low:head_high]
            local_out, state_local = ssd_forward(group_input, b_state, c_state, step_size[..., head_low:head_high], log_decay[..., head_low:head_high], doc_block)
            entry_decay, carry_decay = small_tables(log_decay[..., head_low:head_high], doc_block)
            state_in = forward_chain(carry_decay, state_local)
            state_bf = state_in.astype(jnp.bfloat16)
            cross_term = entry_decay[..., None] * contract('ctn,chpn->cthp', c_state, state_bf)
            outputs.append(local_out + cross_term + d_skip[head_low:head_high, None] * group_input.astype(jnp.float32))
            kept_state.append((entry_decay, carry_decay, state_in, state_bf))
        ssd_flat = jnp.concatenate(outputs, axis=2).reshape(L, inner_width)
        gate_float = gate_proj.astype(jnp.float32)
        gate_sigm = jax.nn.sigmoid(gate_float)
        gated = ssd_flat * gate_float * gate_sigm
        inverse_gate = lax.rsqrt(lax.optimization_barrier(jnp.mean(gated * gated, axis=-1, keepdims=True)) + epsilon)
        gate_normed = (gated * inverse_gate * gain_gate).astype(jnp.bfloat16)
        mixed_out = hidden_float
        for group_index in range(groups):
            channel_low = group_index * group_width
            partial_out = jnp.dot(gate_normed[:, channel_low:channel_low + group_width], w_out[channel_low:channel_low + group_width], preferred_element_type=jnp.float32)
            mixed_out = mixed_out + lax.optimization_barrier(partial_out.astype(jnp.bfloat16)).astype(jnp.float32)
        block_out = mixed_out.astype(jnp.bfloat16)
        cotangent_float = cotangent.astype(jnp.float32)
        grad_out_w = jnp.dot(gate_normed.T, cotangent, preferred_element_type=jnp.float32)
        normed_grad = jnp.dot(cotangent, w_out.T, preferred_element_type=jnp.float32)
        grad_gate_gain = lax.optimization_barrier(jnp.sum(normed_grad * gated * inverse_gate, axis=0))
        scaled = normed_grad * gain_gate
        gate_dot = lax.optimization_barrier(jnp.sum(scaled * gated, axis=-1, keepdims=True))
        gated_grad = inverse_gate * scaled - gated * inverse_gate * inverse_gate * inverse_gate * gate_dot / inner_width
        ssd_grad = gated_grad * gate_float * gate_sigm
        gate_grad = gated_grad * ssd_flat * silu_slope(gate_float, gate_sigm)
        ssd_grad_heads = ssd_grad.reshape(blocks, POS_DEV, H, P_SIZE)
        grad_bf = ssd_grad_heads.astype(jnp.bfloat16)
        grad_skip = lax.optimization_barrier(jnp.sum(ssd_grad_heads * ssd_input.astype(jnp.float32), axis=(0, 1, 3)))
        input_grads = []
        step_grads = []
        log_grads = []
        bc_grads = []
        for group_index in range(groups):
            head_low = group_index * group_heads
            head_high = head_low + group_heads
            entry_decay, carry_decay, state_in, state_bf = kept_state[group_index]
            group_grad = grad_bf[:, :, head_low:head_high]
            grad_local = state_entry_grad(group_grad, c_state, entry_decay)
            grad_out_state = backward_chain(carry_decay, grad_local)
            grad_input, grad_bstate, grad_cstate, grad_step, grad_log = ssd_backward(ssd_input[:, :, head_low:head_high], b_state, c_state, step_size[..., head_low:head_high], log_decay[..., head_low:head_high], doc_block, group_grad, state_bf, state_in, grad_out_state)
            input_grads.append(grad_input + d_skip[head_low:head_high, None] * ssd_grad_heads[:, :, head_low:head_high])
            step_grads.append(grad_step)
            log_grads.append(grad_log)
            bc_grads.append(jnp.concatenate([grad_bstate, grad_cstate], axis=-1).reshape(L, 2 * N))
        grad_log_all = jnp.concatenate(log_grads, axis=2)
        grad_step_all = jnp.concatenate(step_grads, axis=2) - grad_log_all * decay_rates
        grad_alog = lax.optimization_barrier(jnp.sum(grad_log_all * log_decay, axis=(0, 1)))
        raw_grad = grad_step_all * jax.nn.sigmoid(raw_float)
        grad_bias_dt = lax.optimization_barrier(jnp.sum(raw_grad, axis=(0, 1)))
        act_slope = silu_slope(conv_out, conv_sigm)
        x_upstream = jnp.concatenate(input_grads, axis=2).reshape(L, inner_width) * act_slope[:, :inner_width]
        back_x, taps_x_grad, offset_x_grad = conv_backward(padded[:, :, :inner_width], doc_pad, doc_full, conv_weight[:, :inner_width], x_upstream[None])
        bc_upstream = jnp.stack(bc_grads) * act_slope[None, :, inner_width:]
        padded_bc = jnp.broadcast_to(padded[:, :, inner_width:], (groups, L + K - 1, 2 * N))
        back_bc, taps_bc_grad, offset_bc_grad = conv_backward(padded_bc, jnp.broadcast_to(doc_pad, (groups, L + K - 1)), jnp.broadcast_to(doc_full, (groups, L)), conv_weight[:, inner_width:], bc_upstream)
        gate_grad_bf = gate_grad.astype(jnp.bfloat16)
        input_grad_bf = back_x[0, K - 1:].astype(jnp.bfloat16)
        step_grad_bf = raw_grad.reshape(L, H).astype(jnp.bfloat16)
        state_grad_bf = back_bc[:, K - 1:].astype(jnp.bfloat16)
        grad_wz = jnp.dot(normed.T, gate_grad_bf, preferred_element_type=jnp.float32)
        grad_wx = jnp.dot(normed.T, input_grad_bf, preferred_element_type=jnp.float32)
        grad_wdt = jnp.dot(normed.T, step_grad_bf, preferred_element_type=jnp.float32)
        back_in = jnp.dot(gate_grad_bf, w_z.T, preferred_element_type=jnp.float32)
        back_in = back_in + jnp.dot(input_grad_bf, w_x.T, preferred_element_type=jnp.float32)
        back_in = back_in + jnp.dot(step_grad_bf, w_dt.T, preferred_element_type=jnp.float32)
        grad_wbc = jnp.zeros((D, 2 * N), jnp.float32)
        for group_index in range(groups):
            grad_wbc = grad_wbc + jnp.dot(normed.T, state_grad_bf[group_index], preferred_element_type=jnp.float32)
            back_in = back_in + jnp.dot(state_grad_bf[group_index], w_bc.T, preferred_element_type=jnp.float32)
        grad_gain_in = lax.optimization_barrier(jnp.sum(back_in * hidden_float * inverse_rms, axis=0))
        scaled_in = back_in * gain_in
        input_dot = lax.optimization_barrier(jnp.sum(scaled_in * hidden_float, axis=-1, keepdims=True))
        hidden_grad = cotangent_float + inverse_rms * scaled_in - hidden_float * inverse_rms * inverse_rms * inverse_rms * input_dot / D
        step_totals = (grad_gain_in, grad_wz, grad_wx, grad_wbc, grad_wdt, taps_x_grad, offset_x_grad, taps_bc_grad, offset_bc_grad, grad_bias_dt, grad_alog, grad_skip, grad_gate_gain, grad_out_w)
        new_totals = tuple((total + added for total, added in zip(totals, step_totals)))
        return (new_totals, (block_out, hidden_grad))
    start_totals = (jnp.zeros((D,), jnp.float32), jnp.zeros((D, inner_width), jnp.float32), jnp.zeros((D, inner_width), jnp.float32), jnp.zeros((D, 2 * N), jnp.float32), jnp.zeros((D, H), jnp.float32), jnp.zeros((K, inner_width), jnp.float32), jnp.zeros((inner_width,), jnp.float32), jnp.zeros((K, 2 * N), jnp.float32), jnp.zeros((2 * N,), jnp.float32), jnp.zeros((H,), jnp.float32), jnp.zeros((H,), jnp.float32), jnp.zeros((H,), jnp.float32), jnp.zeros((inner_width,), jnp.float32), jnp.zeros((inner_width, D), jnp.float32))
    totals, stacked = lax.scan(per_sequence, start_totals, (hidden_in, out_grad, doc_starts))
    block_out, hidden_grad = stacked
    return (block_out, hidden_grad, totals[0], totals[1], totals[2], totals[3], totals[4], totals[5].reshape(K, H, P_SIZE), totals[6].reshape(H, P_SIZE), totals[7], totals[8], totals[9], totals[10], totals[11], totals[12].reshape(H, P_SIZE), totals[13])
```

```python
import functools

import jax
import jax.numpy as jnp
from jax import lax
from jax.experimental import pallas as pl
from jax.experimental.pallas import tpu as pltpu
from jax.sharding import PartitionSpec as P


epsilon = 1e-05
f32, bf16 = jnp.float32, jnp.bfloat16
LANES = 128
PAD_ROWS = 16
HEAD_ROWS = 16
CUM, ENTRY, SPREAD, STEP, TAIL, FLAGS, SIGM, DECAY = (HEAD_ROWS * i for i in range(8))


def rotated(block, axis, distance):
    size = lax.axis_size(axis)
    return lax.ppermute(block, axis, [(i, (i + distance) % size) for i in range(size)])


def swapped(block, axis, bit):
    size = lax.axis_size(axis)
    return lax.ppermute(block, axis, [(i, i ^ bit) for i in range(size)])


def shifted(block, axis, distance):
    devices = range(lax.axis_size(axis))
    route = [(i, i + distance) for i in devices if i + distance in devices]
    return lax.ppermute(block, axis, route)


def bits_of(axis):
    size = lax.axis_size(axis)
    return [1 << k for k in range(size.bit_length() - 1)]


def gather_line(block, axis):
    size, here = lax.axis_size(axis), lax.axis_index(axis)
    parts = [block] + [rotated(block, axis, k) for k in range(1, size)]
    whole = jnp.zeros((size,) + block.shape, block.dtype)
    for k, part in enumerate(parts):
        whole = lax.dynamic_update_index_in_dim(whole, part, (here - k) % size, 0)
    return whole


def gather_bits(block, axis, order):
    here, done = lax.axis_index(axis), []
    for bit in order:
        other = swapped(block, axis, bit)
        at = sum(1 for b in done if b > bit)
        upper = (here & bit) != 0
        block = jnp.where(
            upper, jnp.stack([other, block], at), jnp.stack([block, other], at)
        )
        done.append(bit)
    return block


def scatter_bits(block, axis, order):
    here, left = lax.axis_index(axis), sorted(order, reverse=True)
    for bit in order:
        at = left.index(bit)
        mine = ((here & bit) != 0).astype(jnp.int32)
        keep = lax.dynamic_index_in_dim(block, mine, at, keepdims=False)
        give = lax.dynamic_index_in_dim(block, 1 - mine, at, keepdims=False)
        got = swapped(give.astype(bf16), axis, bit)
        block = (keep.astype(f32) + got.astype(f32)).astype(bf16)
        left.remove(bit)
    return block


def scatter_line(block, axis):
    size, here = lax.axis_size(axis), lax.axis_index(axis)
    total = lax.dynamic_index_in_dim(block, here, 0, keepdims=False).astype(f32)
    got = [
        rotated(
            lax.dynamic_index_in_dim(block, (here + k) % size, 0, keepdims=False), axis, k
        )
        for k in range(1, size)
    ]
    for part in got:
        total = total + part.astype(f32)
    return total


def gather_pair(first, second):
    ascending = bits_of("dp")
    a = gather_bits(first, "dp", ascending[::-1])
    b = gather_bits(second, "dp", ascending)
    return a, b


def scatter_pair(first, second):
    ascending = bits_of("dp")
    split = (2,) * len(ascending)
    n_line = lax.axis_size("seq")
    first = first.reshape(split + (n_line,) + first.shape[1:])
    second = second.reshape(split + (n_line,) + second.shape[1:])
    a = scatter_bits(first, "dp", ascending)
    b = scatter_bits(second, "dp", ascending[::-1])
    return scatter_line(a, "seq"), scatter_line(b, "seq")


def partner(value):
    return swapped(value, "heads", 1)


def mm(a, b, ca=1, cb=0):
    return lax.dot_general(a, b, (((ca,), (cb,)), ((), ())), preferred_element_type=f32)


def iota(shape, dim):
    return lax.broadcasted_iota(jnp.int32, shape, dim)


def exact_rows(value, table):
    high = value.astype(bf16)
    rest = value - high.astype(f32)
    mid = rest.astype(bf16)
    low = (rest - mid.astype(f32)).astype(bf16)
    rows = value.shape[0]
    out = mm(jnp.concatenate([high, mid, low], 0), table)
    return out[:rows] + out[rows : 2 * rows] + out[2 * rows : 3 * rows]


def selector(offset, inner, head_size):
    shape = (LANES, inner)
    return (iota(shape, 0) - offset == iota(shape, 1) // head_size).astype(bf16)


def head_mask(inner, head_size):
    shape = (HEAD_ROWS, inner)
    return iota(shape, 0) == iota(shape, 1) // head_size


def sigmoid(value):
    return 1.0 / (1.0 + jnp.exp(-value))


def softplus(value):
    return jnp.maximum(value, 0.0) + jnp.log1p(jnp.exp(-jnp.abs(value)))


def conv_sources(pre, taps_of, flags, tap_count):
    rows = PAD_ROWS
    sources = [pre[rows:]]
    out = taps_of(tap_count - 1) * sources[0] + taps_of(tap_count)
    for j in range(1, tap_count):
        source = pltpu.roll(pre, j, 0)[rows:]
        sources.append(source)
        out = out + taps_of(tap_count - 1 - j) * (source * flags[j])
    return out, sources


def project_kernel(
    hid_ref,
    rim_ref,
    start_ref,
    gain_ref,
    w_ref,
    taps_ref,
    head_ref,
    normed_ref,
    pre_ref,
    act_ref,
    row_ref,
    col_ref,
    state_ref,
    carry_ref,
    *,
    inner,
    state,
    tap_count,
    head_size,
):
    length = hid_ref.shape[0]
    chan = inner + 2 * state
    gain = gain_ref[...].astype(f32)

    def norm(v):
        v = v.astype(f32)
        scale = lax.rsqrt(jnp.mean(v * v, axis=-1, keepdims=True) + epsilon)
        return (v * scale * gain).astype(bf16)

    normed = norm(hid_ref[...])
    normed_ref[...] = normed
    proj = mm(jnp.concatenate([norm(rim_ref[...]), normed], 0), w_ref[...])
    pre_ref[...] = proj[:, :chan].astype(bf16)
    raw = proj[PAD_ROWS:, chan:].astype(bf16).astype(f32)
    raw = raw.T[:HEAD_ROWS] + head_ref[:, 0:1]
    step = softplus(raw)
    decay = -step * jnp.exp(head_ref[:, 1:2])
    square = (length, length)
    upper = (iota(square, 0) <= iota(square, 1)).astype(bf16)
    cum = exact_rows(decay, upper)
    start = jnp.broadcast_to(start_ref[...], (HEAD_ROWS, length)).astype(bf16)
    doc = mm(start, upper)
    cum_end = cum[:, length - 1 :]
    fresh = (doc == 0.0).astype(f32)
    closing = (doc == doc[:, length - 1 :]).astype(f32)
    entry = jnp.exp(cum) * fresh
    tail = jnp.exp(cum_end - cum) * closing
    carry = jnp.exp(cum_end) * fresh[:, length - 1 :]
    flag_row = iota((HEAD_ROWS, length), 0)
    lane = iota((HEAD_ROWS, length), 1)
    flags = doc
    for j in range(1, tap_count):
        source = jnp.where(lane < j, 0.0, pltpu.roll(doc, j, 1))
        flags = jnp.where(flag_row == j, (source == doc).astype(f32), flags)
    table = jnp.concatenate(
        [cum, entry, tail * step, step, tail, flags, sigmoid(raw), decay], 0
    )
    row_ref[...] = table
    col = table.T
    col_ref[...] = col
    flag_cols = [None] + [
        jnp.broadcast_to(col[:, FLAGS + j : FLAGS + j + 1], (length, LANES))
        for j in range(1, tap_count)
    ]

    def conv_step(i, carried):
        at = pl.ds(pl.multiple_of(i * LANES, LANES), LANES)
        out, _ = conv_sources(
            pre_ref[:, at].astype(f32), lambda k: taps_ref[k : k + 1, at], flag_cols, tap_count
        )
        act_ref[:, at] = (out * sigmoid(out)).astype(bf16)
        return carried

    lax.fori_loop(0, chan // LANES, conv_step, 0)
    spread = mm(col.astype(bf16), selector(SPREAD, inner, head_size))
    weighted = (act_ref[:, :inner].astype(f32) * spread).astype(bf16)
    state_ref[...] = mm(act_ref[:, inner : inner + state], weighted, 0, 0).astype(bf16)
    carry_ref[...] = jnp.sum(
        jnp.where(head_mask(inner, head_size), carry, 0.0), axis=0, keepdims=True
    )


def linked_of(row_ref, col_ref, first, second):
    doc_row = row_ref[FLAGS : FLAGS + 1, :]
    doc_col = col_ref[:, FLAGS : FLAGS + 1]
    return (doc_row == doc_col) & (first >= second)


def column(col_ref, index):
    return pltpu.roll(col_ref[...], (2 * LANES - index) % LANES, 1)[:, 0:1]


def local_kernel(act_ref, row_ref, col_ref, out_ref, *, inner, state, head_size):
    length = act_ref.shape[0]
    square = (length, length)
    per = LANES // head_size
    b, c = act_ref[:, inner : inner + state], act_ref[:, inner + state :]
    linked = linked_of(row_ref, col_ref, iota(square, 0), iota(square, 1))
    inner_prod = jnp.where(linked, mm(c, b, 1, 1), 0.0)
    half = iota((length, LANES), 1) // head_size

    def pair(i, carried):
        at = pl.ds(pl.multiple_of(i * LANES, LANES), LANES)
        x = act_ref[:, at]
        out = jnp.zeros((length, LANES), f32)
        for q in range(per):
            h = i * per + q
            spread = column(col_ref, h + CUM) - row_ref[pl.ds(h + CUM, 1), :]
            decays = jnp.exp(jnp.minimum(spread, 0.0))
            scores = (inner_prod * decays * row_ref[pl.ds(h + STEP, 1), :]).astype(bf16)
            out = out + mm(scores, jnp.where(half == q, x, jnp.zeros_like(x)))
        out_ref[:, at] = out.astype(bf16)
        return carried

    lax.fori_loop(0, inner // LANES, pair, 0)


def mix_kernel(
    normed_ref,
    act_ref,
    local_ref,
    col_ref,
    state_ref,
    cot_ref,
    wz_ref,
    wo_ref,
    skip_ref,
    gain_ref,
    gate_ref,
    ssd_ref,
    ng_ref,
    sum_ref,
    *,
    inner,
    state,
    head_size,
):
    length = act_ref.shape[0]
    gate = mm(normed_ref[...], wz_ref[...]).astype(bf16)
    gate_ref[...] = gate
    normed_grad = mm(cot_ref[...], wo_ref[...]).astype(bf16)
    ng_ref[...] = normed_grad
    cross = mm(act_ref[:, inner + state :], state_ref[...])
    entry = mm(col_ref[...].astype(bf16), selector(ENTRY, inner, head_size))
    ssd = (
        local_ref[...].astype(f32)
        + entry * cross
        + skip_ref[...] * act_ref[:, :inner].astype(f32)
    ).astype(bf16)
    ssd_ref[...] = ssd
    gate = gate.astype(f32)
    gated = ssd.astype(f32) * gate * sigmoid(gate)
    squares = jnp.sum(gated * gated, axis=1, keepdims=True)
    dots = jnp.sum(normed_grad.astype(f32) * gain_ref[...] * gated, axis=1, keepdims=True)
    lane = iota((length, LANES), 1)
    sums = jnp.where(lane == 0, squares, jnp.where(lane == 1, dots, 0.0))
    sum_ref[...] = sums.T[: sum_ref.shape[0]]


def gate_kernel(
    total_ref,
    gate_ref,
    ssd_ref,
    ng_ref,
    act_ref,
    col_ref,
    wo_ref,
    gain_ref,
    gn_ref,
    part_ref,
    gg_ref,
    grad_ref,
    state_ref,
    sum_ref,
    *,
    inner,
    state,
    head_size,
    inner_total,
):
    length = act_ref.shape[0]
    total = total_ref[...]
    inverse = lax.rsqrt(total[0:1] / inner_total + epsilon)
    pull = inverse * inverse * inverse * total[1:2] / inner_total
    rows = iota((LANES, length), 0)
    cols = jnp.where(rows == 0, inverse, jnp.where(rows == 1, pull, 0.0)).T
    inverse, pull = cols[:, 0:1], cols[:, 1:2]
    gate = gate_ref[...].astype(f32)
    ssd = ssd_ref[...].astype(f32)
    normed_grad = ng_ref[...].astype(f32)
    sig = sigmoid(gate)
    act = gate * sig
    gated = ssd * act
    gain = gain_ref[...]
    unit = gated * inverse
    gate_normed = (unit * gain).astype(bf16)
    gn_ref[...] = gate_normed
    part_ref[...] = mm(gate_normed, wo_ref[...], 1, 1).astype(bf16)
    gated_grad = inverse * (normed_grad * gain) - gated * pull
    ssd_grad = gated_grad * act
    gg_ref[...] = (gated_grad * ssd * (sig * (1.0 + gate * (1.0 - sig)))).astype(bf16)
    grad_bf = ssd_grad.astype(bf16)
    grad_ref[...] = grad_bf
    entry = mm(col_ref[...].astype(bf16), selector(ENTRY, inner, head_size))
    entered = (entry * grad_bf.astype(f32)).astype(bf16)
    state_ref[...] = mm(act_ref[:, inner + state :], entered, 0, 0).astype(bf16)
    gain_sum = jnp.sum(normed_grad * unit, axis=0, keepdims=True)
    skip_sum = jnp.sum(ssd_grad * act_ref[:, :inner].astype(f32), axis=0, keepdims=True)
    row = iota((8, inner), 0)
    sums = jnp.where(row == 0, gain_sum, jnp.where(row == 1, skip_sum, 0.0))

    @pl.when(pl.program_id(0) == 0)
    def _():
        sum_ref[...] = jnp.zeros_like(sum_ref)

    sum_ref[...] += sums


def intra_kernel(
    act_ref, grad_ref, row_ref, col_ref, gi_ref, bc_ref, stat_ref, acc_ref, q_ref, *, inner, state, head_size
):
    length = act_ref.shape[0]
    square = (length, length)
    per = LANES // head_size
    b, c = act_ref[:, inner : inner + state], act_ref[:, inner + state :]
    linked = linked_of(row_ref, col_ref, iota(square, 1), iota(square, 0))
    inner_prod = jnp.where(linked, mm(b, c, 1, 1), 0.0)
    lane = iota((length, LANES), 1)
    half = lane // head_size
    acc_ref[...] = jnp.zeros_like(acc_ref)
    q_ref[...] = jnp.zeros_like(q_ref)

    def pair(i, carried):
        at = pl.ds(pl.multiple_of(i * LANES, LANES), LANES)
        x, g = act_ref[:, at], grad_ref[:, at]
        out = jnp.zeros((length, LANES), f32)
        for q in range(per):
            h = i * per + q
            step = column(col_ref, h + STEP)
            spread = row_ref[pl.ds(h + CUM, 1), :] - column(col_ref, h + CUM)
            decays = jnp.exp(jnp.minimum(spread, 0.0))
            g_half = jnp.where(half == q, g, jnp.zeros_like(g))
            masked = mm(x, g_half, 1, 1) * decays
            acc_ref[...] += masked * step
            part = masked * inner_prod
            stat_ref[pl.ds(h, 1), :] = jnp.sum(part * step, axis=0, keepdims=True)
            q_ref[...] += jnp.where(lane == h, jnp.sum(part, axis=1, keepdims=True), 0.0)
            scores = (inner_prod * decays * step).astype(bf16)
            out = out + mm(scores, g_half)
        gi_ref[:, at] = out.astype(bf16)
        return carried

    lax.fori_loop(0, inner // LANES, pair, 0)
    stat_ref[HEAD_ROWS:, :] = q_ref[...].T[:HEAD_ROWS]
    inner_grad = jnp.where(linked, acc_ref[...], 0.0).astype(bf16)
    bc_ref[:, :state] = mm(inner_grad, c)
    bc_ref[:, state:] = mm(inner_grad, b, 0, 0)


def finish_kernel(
    act_ref,
    pre_ref,
    grad_ref,
    row_ref,
    col_ref,
    gi_ref,
    bc_ref,
    stat_ref,
    state_ref,
    gstate_ref,
    carry_ref,
    taps_ref,
    head_ref,
    skip_ref,
    comb_ref,
    rim_ref,
    tapg_ref,
    scal_ref,
    up_ref,
    *,
    inner,
    state,
    heads,
    tap_count,
    head_size,
):
    length = act_ref.shape[0]
    chan = inner + 2 * state

    @pl.when(pl.program_id(0) == 0)
    def _():
        tapg_ref[...] = jnp.zeros_like(tapg_ref)
        scal_ref[...] = jnp.zeros_like(scal_ref)

    x = act_ref[:, :inner].astype(f32)
    b, c = act_ref[:, inner : inner + state], act_ref[:, inner + state :]
    grad = grad_ref[...].astype(f32)
    state_in, gstate = state_ref[...], gstate_ref[...]
    col_bf = col_ref[...].astype(bf16)
    spread = mm(col_bf, selector(SPREAD, inner, head_size))
    entry = mm(col_bf, selector(ENTRY, inner, head_size))
    back = mm(b, gstate)
    cross = mm(c, state_in)
    up_ref[:, :inner] = gi_ref[...].astype(f32) + spread * back + skip_ref[...] * grad
    up_ref[:, inner : inner + state] = bc_ref[:, :state] + mm(
        (spread * x).astype(bf16), gstate, 1, 1
    )
    up_ref[:, inner + state :] = bc_ref[:, state:] + mm(
        (entry * grad).astype(bf16), state_in, 1, 1
    )
    mask = head_mask(inner, head_size)
    mask_bf = mask.astype(bf16)
    dot_b = mm(mask_bf, (x * back).astype(bf16), 1, 1)
    dot_c = mm(mask_bf, (grad * cross).astype(bf16), 1, 1)
    row = lambda at: row_ref[at : at + HEAD_ROWS, :]
    kept = stat_ref[HEAD_ROWS:, :]
    spent = dot_b * row(SPREAD)
    cum_grad = row(ENTRY) * dot_c + stat_ref[:HEAD_ROWS, :] - row(STEP) * kept - spent
    across = carry_ref[...] * jnp.sum(
        gstate.astype(f32) * state_in.astype(f32), axis=0, keepdims=True
    )
    end = jnp.sum(spent, axis=1, keepdims=True) + jnp.sum(
        jnp.where(mask, across, 0.0), axis=1, keepdims=True
    )
    lane = iota((HEAD_ROWS, length), 1)
    cum_grad = cum_grad + jnp.where(lane == length - 1, end, 0.0)
    square = (length, length)
    lower = (iota(square, 0) >= iota(square, 1)).astype(bf16)
    log_grad = exact_rows(cum_grad, lower)
    step_grad = kept + dot_b * row(TAIL) - log_grad * jnp.exp(head_ref[:, 1:2])
    raw_grad = step_grad * row(SIGM)
    raw_grad = jnp.where(iota((HEAD_ROWS, length), 0) < heads, raw_grad, 0.0)
    raw_sum = jnp.sum(raw_grad, axis=1, keepdims=True)
    log_sum = jnp.sum(log_grad * row(DECAY), axis=1, keepdims=True)
    at_lane = iota((HEAD_ROWS, LANES), 1)
    scal_ref[...] += jnp.where(at_lane == 0, raw_sum, jnp.where(at_lane == 1, log_sum, 0.0))
    filler = jnp.zeros((LANES - HEAD_ROWS, length), f32)
    comb_ref[:, chan:] = jnp.concatenate([raw_grad, filler], 0).T.astype(bf16)
    flag_cols = [None] + [
        jnp.broadcast_to(col_ref[:, FLAGS + j : FLAGS + j + 1], (length, LANES))
        for j in range(1, tap_count)
    ]
    above = jnp.zeros((PAD_ROWS, LANES), f32)

    def conv_step(i, carried):
        at = pl.ds(pl.multiple_of(i * LANES, LANES), LANES)
        taps_of = lambda k: taps_ref[k : k + 1, at]
        out, sources = conv_sources(pre_ref[:, at].astype(f32), taps_of, flag_cols, tap_count)
        sig = sigmoid(out)
        grads = up_ref[:, at] * (sig * (1.0 + out * (1.0 - sig)))
        tapg_ref[tap_count : tap_count + 1, at] += jnp.sum(grads, axis=0, keepdims=True)
        result = jnp.concatenate([above, grads * taps_of(tap_count - 1)], 0)
        for j in range(tap_count):
            masked = grads * flag_cols[j] if j else grads
            k = tap_count - 1 - j
            tapg_ref[k : k + 1, at] += jnp.sum(masked * sources[j], axis=0, keepdims=True)
            if j:
                placed = jnp.concatenate([above, masked * taps_of(k)], 0)
                result = result + pltpu.roll(placed, length + PAD_ROWS - j, 0)
        rim_ref[:, at] = result[:PAD_ROWS].astype(bf16)
        comb_ref[:, at] = result[PAD_ROWS:].astype(bf16)
        return carried

    lax.fori_loop(0, chan // LANES, conv_step, 0)


def per_seq(*shape):
    return pl.BlockSpec((None,) + shape, lambda i: (i,) + (0,) * len(shape))


def fixed(*shape):
    return pl.BlockSpec(shape, lambda i: (0,) * len(shape))


def run(kernel, seqs, args, in_specs, outs, scratch=(), **names):
    return pl.pallas_call(
        functools.partial(kernel, **names),
        grid=(seqs,),
        in_specs=in_specs,
        out_specs=[o[0] for o in outs],
        out_shape=[jax.ShapeDtypeStruct(o[1], o[2]) for o in outs],
        scratch_shapes=list(scratch),
        compiler_params=pltpu.CompilerParams(
            dimension_semantics=("arbitrary",), vmem_limit_bytes=60000 * 1024
        ),
        name=kernel.__name__,
    )(*args)


def placed(value, rows, row, lane, lanes=LANES):
    lead = ((0, 0, 0),) * (value.ndim - 2)
    high = lead + (
        (row, rows - row - value.shape[-2], 0),
        (lane, lanes - lane - value.shape[-1], 0),
    )
    return lax.pad(value, jnp.zeros((), value.dtype), high)


def chain(local, carry, reverse):
    size = lax.axis_size("seq")
    results = []
    for s in range(local.shape[0]):
        own, factor = local[s], carry[s]
        give, total = own, None
        for hop in range(size - 1):
            pair = (size - 1 - hop, size - 2 - hop) if reverse else (hop, hop + 1)
            got = lax.ppermute(give, "seq", [pair])
            total = got if total is None else total + got
            give = (own.astype(f32) + factor * got.astype(f32)).astype(bf16)
        results.append(total)
    return jnp.stack(results)


def shards(
    hidden_in,
    out_grad,
    doc_starts,
    norm_gain,
    w_z,
    w_x,
    w_bc,
    w_dt,
    conv_x,
    conv_bias_x,
    conv_bc,
    conv_bias_bc,
    dt_bias,
    a_log,
    d_skip,
    gated_gain,
    w_out,
):
    seqs, length, width = hidden_in.shape
    heads = dt_bias.shape[0]
    inner = w_x.shape[1]
    head_size = inner // heads
    taps = conv_x.shape[0]
    state = w_bc.shape[1] // 2
    chan = inner + 2 * state
    groups = lax.axis_size("heads")
    here = lax.axis_index("heads")
    sources = lax.axis_size("dp") * lax.axis_size("seq")
    rows = w_x.shape[0]
    bc_rows = w_bc.shape[0]
    j_x = conv_x.shape[2]
    j_gain, j_bc = norm_gain.shape[0], conv_bc.shape[1]
    l_cx = HEAD_ROWS
    l_cb = l_cx + taps * j_x
    l_gg = l_cb + j_x
    l_ng = l_gg + j_x
    l_tb = l_ng + j_gain
    l_bb = l_tb + j_bc

    rim = taps - 1
    rim_mask = jnp.stack(
        [jnp.sum(doc_starts[:, length - rim + 1 + i :], axis=1) == 0 for i in range(rim)], 1
    ).astype(bf16)[..., None]
    rim_rows = shifted(
        jnp.pad(hidden_in[:, length - rim :] * rim_mask, ((0, 0), (PAD_ROWS - rim, 0), (0, 0))),
        "seq",
        1,
    )

    small = placed(w_dt, rows, 0, 0)
    for k in range(taps):
        small = small + placed(conv_x[k], rows, 0, l_cx + k * j_x)
    small = small + placed(conv_bias_x, rows, 0, l_cb) + placed(gated_gain, rows, 0, l_gg)
    small = small + placed(norm_gain[None], rows, 0, l_ng) + placed(conv_bc, rows, 0, l_tb)
    small = small + placed(conv_bias_bc[None], rows, 0, l_bb)
    stacked_bc = jnp.concatenate([w_bc[:, :state], w_bc[:, state:]], axis=0)
    early = jnp.concatenate([w_x, stacked_bc, small], axis=1)
    cut = early.shape[1] // 2
    line = gather_line(early, "seq")
    part_a, part_b = gather_pair(line[..., :cut], line[..., cut:])
    early = jnp.concatenate([part_a, part_b], -1).reshape(sources, rows, -1)
    shared = early[..., inner:]
    other = partner(shared)
    pair = jnp.where(here == 0, jnp.stack([shared, other], 1), jnp.stack([other, shared], 1))
    full_bc = pair[..., :state].reshape(sources, groups, 2, bc_rows, state)
    full_bc = jnp.transpose(full_bc, (0, 1, 3, 2, 4)).reshape(width, 2 * state)
    own_small = shared[..., state:]
    full_dt = own_small.reshape(width, LANES)
    full_w = jnp.concatenate([early[..., :inner].reshape(width, inner), full_bc, full_dt], 1)
    vectors = own_small[:, :heads, l_cx:l_ng].reshape(sources, heads, taps + 2, j_x)
    vectors = jnp.transpose(vectors, (2, 1, 0, 3)).reshape(taps + 2, inner).astype(f32)
    pair_small = pair[..., state:]
    gain_in = pair_small[:, :, 0, l_ng:l_tb].reshape(1, width)
    taps_bc = jnp.transpose(pair_small[:, :, :taps, l_tb:l_bb], (2, 0, 1, 3)).reshape(taps, -1)
    bias_bc = pair_small[:, :, 0, l_bb : l_bb + j_bc].reshape(1, -1)
    vectors_bc = jnp.concatenate([taps_bc, bias_bc], 0).astype(f32)
    conv_table = jnp.concatenate([vectors[: taps + 1], vectors_bc], 1)
    conv_table = jnp.pad(conv_table, ((0, -(taps + 1) % 8), (0, 0)))
    gain_gate = vectors[taps + 1 :]

    late = gather_line(jnp.stack([w_z, w_out.T]), "seq")
    full_z, full_o = gather_pair(late[:, 0], late[:, 1])
    full_z, full_o = full_z.reshape(width, inner), full_o.reshape(width, inner)

    head_table = jnp.pad(
        jnp.stack([dt_bias, a_log], 1), ((0, HEAD_ROWS - heads), (0, LANES - 2))
    )
    skip_row = jnp.repeat(d_skip, head_size)[None]
    starts = doc_starts.astype(f32)[:, None]
    sizes = dict(inner=inner, state=state, head_size=head_size)
    seq = lambda r, c, kind: (per_seq(r, c), (seqs, r, c), kind)

    normed, pre, act, row_tab, col_tab, state_local, carry = run(
        project_kernel,
        seqs,
        (hidden_in, rim_rows, starts, gain_in, full_w, conv_table, head_table),
        [
            per_seq(length, width),
            per_seq(PAD_ROWS, width),
            per_seq(1, length),
            fixed(1, width),
            fixed(*full_w.shape),
            fixed(*conv_table.shape),
            fixed(HEAD_ROWS, LANES),
        ],
        [
            seq(length, width, bf16),
            seq(length + PAD_ROWS, chan, bf16),
            seq(length, chan, bf16),
            seq(LANES, length, f32),
            seq(length, LANES, f32),
            seq(state, inner, bf16),
            seq(1, inner, f32),
        ],
        tap_count=taps,
        **sizes,
    )
    state_in = chain(state_local, carry, False)
    (local_out,) = run(
        local_kernel,
        seqs,
        (act, row_tab, col_tab),
        [per_seq(length, chan), per_seq(LANES, length), per_seq(length, LANES)],
        [seq(length, inner, bf16)],
        **sizes,
    )
    gate, ssd_out, normed_grad, sums = run(
        mix_kernel,
        seqs,
        (normed, act, local_out, col_tab, state_in, out_grad, full_z, full_o, skip_row, gain_gate),
        [
            per_seq(length, width),
            per_seq(length, chan),
            per_seq(length, inner),
            per_seq(length, LANES),
            per_seq(state, inner),
            per_seq(length, width),
            fixed(width, inner),
            fixed(width, inner),
            fixed(1, inner),
            fixed(1, inner),
        ],
        [
            seq(length, inner, bf16),
            seq(length, inner, bf16),
            seq(length, inner, bf16),
            seq(8, length, f32),
        ],
        **sizes,
    )
    totals = sums + partner(sums)
    gate_normed, part_out, gate_grad, grad_bf, grad_local, gate_sums = run(
        gate_kernel,
        seqs,
        (totals, gate, ssd_out, normed_grad, act, col_tab, full_o, gain_gate),
        [
            per_seq(8, length),
            per_seq(length, inner),
            per_seq(length, inner),
            per_seq(length, inner),
            per_seq(length, chan),
            per_seq(length, LANES),
            fixed(width, inner),
            fixed(1, inner),
        ],
        [
            seq(length, inner, bf16),
            seq(length, width, bf16),
            seq(length, inner, bf16),
            seq(length, inner, bf16),
            seq(state, inner, bf16),
            (fixed(8, inner), (8, inner), f32),
        ],
        inner_total=inner * groups,
        **sizes,
    )
    grad_state = chain(grad_local, carry, True)
    grad_in, grad_bc, stats = run(
        intra_kernel,
        seqs,
        (act, grad_bf, row_tab, col_tab),
        [
            per_seq(length, chan),
            per_seq(length, inner),
            per_seq(LANES, length),
            per_seq(length, LANES),
        ],
        [
            seq(length, inner, bf16),
            seq(length, 2 * state, f32),
            seq(2 * HEAD_ROWS, length, f32),
        ],
        scratch=[pltpu.VMEM((length, length), f32), pltpu.VMEM((length, LANES), f32)],
        **sizes,
    )

    width_here = width // groups
    left = lambda v: v[..., :width_here]
    right = lambda v: v[..., width_here:]
    own_half = lambda v: jnp.where(here == 0, left(v), right(v))
    other_half = lambda v: jnp.where(here == 0, right(v), left(v))
    mixed = own_half(part_out).astype(f32) + partner(other_half(part_out)).astype(f32)
    hidden_half = own_half(hidden_in).astype(f32)
    block_out = (hidden_half + mixed).astype(bf16)

    tokens = seqs * length
    flat = lambda v: v.reshape(tokens, -1)
    normed_flat = flat(normed)
    grad_out = mm(flat(out_grad), flat(gate_normed), 0, 0).astype(bf16)
    grad_z = mm(normed_flat, flat(gate_grad), 0, 0).astype(bf16)
    own_z, own_o = scatter_pair(
        grad_z.reshape(sources, rows, inner), grad_out.reshape(sources, rows, inner)
    )

    comb, rim_grad, tap_sums, scal_sums = run(
        finish_kernel,
        seqs,
        (
            act,
            pre,
            grad_bf,
            row_tab,
            col_tab,
            grad_in,
            grad_bc,
            stats,
            state_in,
            grad_state,
            carry,
            conv_table,
            head_table,
            skip_row,
        ),
        [
            per_seq(length, chan),
            per_seq(length + PAD_ROWS, chan),
            per_seq(length, inner),
            per_seq(LANES, length),
            per_seq(length, LANES),
            per_seq(length, inner),
            per_seq(length, 2 * state),
            per_seq(2 * HEAD_ROWS, length),
            per_seq(state, inner),
            per_seq(state, inner),
            per_seq(1, inner),
            fixed(*conv_table.shape),
            fixed(HEAD_ROWS, LANES),
            fixed(1, inner),
        ],
        [
            seq(length, chan + LANES, bf16),
            seq(PAD_ROWS, chan, bf16),
            (fixed(8, chan), (8, chan), f32),
            (fixed(HEAD_ROWS, LANES), (HEAD_ROWS, LANES), f32),
        ],
        scratch=[pltpu.VMEM((length, chan), f32)],
        heads=heads,
        tap_count=taps,
        **sizes,
    )
    came = shifted(rim_grad[:, PAD_ROWS - rim :], "seq", -1) * rim_mask
    comb = comb.at[:, length - rim :, :chan].add(came)

    grad_w = mm(normed_flat, flat(comb), 0, 0)
    back = mm(flat(gate_grad), full_z, 1, 1) + mm(flat(comb), full_w, 1, 1)
    hidden_flat = flat(hidden_in).astype(f32)
    inverse = lax.rsqrt(jnp.mean(hidden_flat * hidden_flat, axis=-1, keepdims=True) + epsilon)
    gain_sum = jnp.sum(back * (hidden_flat * inverse), axis=0)

    to_owner = lambda v, n: v.reshape(v.shape[0], sources, groups, n).transpose(1, 2, 0, 3)
    shared = grad_w[:, inner:chan].reshape(sources, groups, bc_rows, 2 * state)
    span = jnp.concatenate(
        [
            placed(to_owner(gain_sum[None], j_gain), 8, 0, 0, 2 * state)
            + placed(to_owner(tap_sums[: taps + 1, inner:], j_bc), 8, 1, 0, 2 * state)
        ],
        0,
    )
    shared = jnp.concatenate([shared, span], 2)
    keep = lax.dynamic_index_in_dim(shared, here, 1, keepdims=False)
    give = lax.dynamic_index_in_dim(shared, 1 - here, 1, keepdims=False).astype(bf16)
    shared = (keep + partner(give).astype(f32)).astype(bf16)

    vectors = jnp.concatenate([tap_sums[: taps + 1, :inner], gate_sums[:1]], 0)
    vectors = vectors.reshape(taps + 2, heads, sources, j_x).transpose(2, 1, 0, 3)
    vectors = vectors.reshape(sources, heads, (taps + 2) * j_x)
    skip_sum = jnp.sum(gate_sums[1].reshape(heads, head_size), axis=1)
    scalars = jnp.concatenate([scal_sums[:heads, :2], skip_sum[:, None]], 1)
    scalars = jnp.broadcast_to(scalars, (sources, heads, 3))
    l_sc = l_cx + (taps + 2) * j_x
    dt_block = grad_w[:, chan:].reshape(sources, rows, LANES)
    dt_block = (
        jnp.where(iota(dt_block.shape, 2) < heads, dt_block, 0.0)
        + placed(vectors, rows, 0, l_cx)
        + placed(scalars, rows, 0, l_sc)
    )
    own = jnp.concatenate([grad_w[:, :inner].reshape(sources, rows, inner), dt_block], -1)
    own = own.astype(bf16)
    cut = (inner + LANES + LANES) // 2
    rest = own.shape[-1] - cut
    second = jnp.concatenate(
        [own[..., cut:], jnp.pad(shared, ((0, 0), (0, 0), (0, rest - 2 * state)))], 1
    )
    first, second = scatter_pair(own[..., :cut], second)
    own = jnp.concatenate([first, second[:rows]], -1)
    shared = second[rows:, : 2 * state]
    block = own[:, inner:]
    vectors = block[:heads, l_cx:l_sc].reshape(heads, taps + 2, j_x).transpose(1, 0, 2)

    back = back.astype(bf16)
    total = own_half(back).astype(f32) + partner(other_half(back)).astype(f32)
    gain_half = own_half(gain_in).astype(f32)
    hidden_half = hidden_half.reshape(tokens, width_here)
    scaled = total * gain_half
    dots = jnp.sum(scaled * hidden_half, axis=-1).reshape(-1, LANES)
    dots = (dots + partner(dots)).reshape(tokens, 1)
    input_grad = (
        own_half(flat(out_grad)).astype(f32)
        + inverse * scaled
        - hidden_half * (inverse * inverse * inverse * dots / width)
    )
    return (
        block_out,
        input_grad.reshape(seqs, length, width_here),
        shared[bc_rows, :j_gain],
        own_z,
        own[:, :inner],
        shared[:bc_rows],
        block[:, :heads],
        vectors[:taps],
        vectors[taps],
        shared[bc_rows + 1 : bc_rows + 1 + taps, :j_bc],
        shared[bc_rows + 1 + taps, :j_bc],
        block[:heads, l_sc],
        block[:heads, l_sc + 1],
        block[:heads, l_sc + 2],
        vectors[taps + 1],
        own_o.T,
    )


def solution(mesh):
    in_specs = (
        P("dp", "seq", None),
        P("dp", "seq", None),
        P("dp", "seq"),
        P(("dp", "seq", "heads")),
        P(("dp", "seq"), "heads"),
        P(("dp", "seq"), "heads"),
        P(("dp", "seq", "heads"), None),
        P(("dp", "seq"), "heads"),
        P(None, "heads", ("dp", "seq")),
        P("heads", ("dp", "seq")),
        P(None, ("dp", "seq", "heads")),
        P(("dp", "seq", "heads")),
        P("heads"),
        P("heads"),
        P("heads"),
        P("heads", ("dp", "seq")),
        P("heads", ("dp", "seq")),
    )
    out_specs = (
        P("dp", "seq", "heads"),
        P("dp", "seq", "heads"),
        P(("dp", "seq", "heads")),
        P(("dp", "seq"), "heads"),
        P(("dp", "seq"), "heads"),
        P(("dp", "seq", "heads"), None),
        P(("dp", "seq"), "heads"),
        P(None, "heads", ("dp", "seq")),
        P("heads", ("dp", "seq")),
        P(None, ("dp", "seq", "heads")),
        P(("dp", "seq", "heads")),
        P("heads"),
        P("heads"),
        P("heads"),
        P("heads", ("dp", "seq")),
        P("heads", ("dp", "seq")),
    )
    return jax.shard_map(shards, mesh=mesh, in_specs=in_specs, out_specs=out_specs, check_vma=False)
```
